1024 devices in a mesh: tile: 64 (over z, x_hi, core), mem: 16 (over x_lo, y).
Axes of the slice: x: 4 (x_hi: 2, x_lo: 2; x = x_hi * 2 + x_lo), y: 8, z: 16, core: 2. Of those that a mesh axis runs over, the one named last changes fastest.
Arguments:
- right_side: float32 [64, 256, 16, 256], P('tile', 'mem'), may hold values from -6 to 6
- perturbations: bfloat16 [64, 256, 6, 16, 256], P('tile', 'mem'), may hold values from -0.375 to 0.375
- precision: float32 [64, 6, 16, 256], P('tile'), may hold values from 5 to 40
- covered: int32 [64, 2, 16], P('tile'), may hold values 0 or 1
Outputs:
- weights: float32 [64, 256, 16, 256], P('tile', 'mem')
- residual: float32 [64, 256, 16, 256], P('tile', 'mem')
The draws below stay inside these ranges and needn't reach their ends.
All inputs are finite; a program needn't handle non-finite values. No bound on the sum of `covered` on one device may be relied on, other than what follows from the above.
Results may differ from the reference program's by a relative error of at most 0.006.
Values sent between devices are 32-bit elements; how exact they have to be, the bound alone decides.
A program may use at most 32 MiB of HBM per device.

```python
import math
import jax
import jax.numpy as jnp
from jax import lax

TY = 16
TX = 256
TCOLS = 8
VL = 6
MEMBERS = 256
TILES = 64
ITERS = 2


def set_ends(array, own_key, low, largest):
    spot = [jax.random.randint(jax.random.fold_in(own_key, axis), (), 0, length) for axis, length in enumerate(array.shape)]
    main_axis = array.shape.index(max(array.shape))
    neighbour = spot[:main_axis] + [(spot[main_axis] + 1) % array.shape[main_axis]] + spot[main_axis + 1:]
    return array.at[tuple(spot)].set(low).at[tuple(neighbour)].set(largest)


def steps_of(rng, shape, pieces, least, largest):
    def one(position, parts):
        draws = jax.random.uniform(jax.random.fold_in(jax.random.fold_in(rng, 6), position), (parts,), jnp.float32, least / len(pieces), largest / len(pieces))
        return jnp.repeat(jnp.exp(draws), shape[position] // parts).reshape((-1,) + (1,) * (len(shape) - position - 1))

    factor_of = one(*pieces[0])
    for cut in pieces[1:]:
        factor_of = factor_of * one(*cut)
    return factor_of


def scatter_about(key, dims, scale, reach, cuts=(), dtype=jnp.bfloat16):
    loudness = steps_of(key, dims, cuts, -0.22, 0.18) if cuts else 1.0
    values = jax.random.normal(key, dims, jnp.float32) * scale * loudness
    return jnp.minimum(jnp.maximum(values, -reach), reach).astype(dtype)


def setup_inputs(seed: int = 0) -> dict:
    streams_of = jax.random.split(jax.random.key(seed), 5)
    right_side = scatter_about(streams_of[0], (TILES, MEMBERS, TY, TX), 1.0, 6.0, ((0, 64), (1, 16)), jnp.float32)
    perturbations = scatter_about(streams_of[1], (TILES, MEMBERS, VL, TY, TX), MEMBERS ** -0.5, 0.375, ((0, 64), (1, 16)))
    precision = jnp.clip(jnp.exp(math.log(40.0) - 2.0794415 * jax.random.uniform(streams_of[2], (TILES, VL, TY, TX), jnp.float32) ** steps_of(streams_of[2], (TILES, VL, TY, TX), ((0, 64),), -0.2, 0.2)), 5.0, 40.0)
    covered = set_ends((jax.random.randint(streams_of[3], (TILES, TY // 8, TX // 16), 0, 4) < 3).astype(jnp.int32), jax.random.fold_in(streams_of[3], 1), 0, 1)
    return {"right_side": right_side, "perturbations": perturbations, "precision": precision, "covered": covered}


def filter_taps():
    offsets = jnp.arange(-8, 9).astype(jnp.float32)
    raw = jnp.exp(-offsets * offsets / 32.0)
    return raw / jnp.sqrt(jnp.sum(jnp.exp(-offsets * offsets / 16.0)))

def to_grid(field):
    rows = field.shape[0] // TCOLS
    return field.reshape(rows, TCOLS, TY, TX).transpose(0, 2, 1, 3).reshape(rows * TY, TCOLS * TX)

def to_tiles(grid):
    rows = grid.shape[0] // TY
    return grid.reshape(rows, TY, TCOLS, TX).transpose(0, 2, 1, 3).reshape(rows * TCOLS, TY, TX)

def smooth_grid(grid):
    taps = filter_taps()
    height, width = grid.shape
    padded = jnp.pad(grid, ((8, 8), (0, 0)))
    along = jnp.zeros_like(grid)
    for j in range(17):
        along = along + taps[j] * padded[j:j + height, :]
    tile_rows = height // TY
    strip = along.reshape(tile_rows, TY, width).transpose(1, 0, 2).reshape(TY, tile_rows * width)
    length = tile_rows * width
    padded = jnp.pad(strip, ((0, 0), (8, 8)), mode='wrap')
    result = jnp.zeros_like(strip)
    for j in range(17):
        result = result + taps[j] * padded[:, j:j + length]
    return result.reshape(TY, tile_rows, width).transpose(1, 0, 2).reshape(height, width)

def smooth_member(field):
    return to_tiles(smooth_grid(to_grid(field)))

def apply_operator(direction, perturbations, obs_weight):

    def filtered(index):
        return smooth_member(lax.dynamic_index_in_dim(direction, index, 1, keepdims=False))
    smoothed = lax.map(filtered, jnp.arange(MEMBERS))

    def accumulate(index, total):
        member = lax.dynamic_index_in_dim(perturbations, index, 1, keepdims=False).astype(jnp.float32)
        return total + member * smoothed[index][:, None, :, :]
    increment = lax.fori_loop(0, MEMBERS, accumulate, jnp.zeros(obs_weight.shape, jnp.float32))
    weighted = obs_weight * increment

    def adjoint(index):
        member = lax.dynamic_index_in_dim(perturbations, index, 1, keepdims=False).astype(jnp.float32)
        return smooth_member(lax.optimization_barrier(jnp.sum(member * weighted, axis=1)))
    back = jnp.moveaxis(lax.map(adjoint, jnp.arange(MEMBERS)), 0, 1)
    return direction + back

def reference(right_side, perturbations, precision, covered):
    mask = covered.astype(jnp.float32)
    tiles_count = precision.shape[0]
    obs_weight = (precision.reshape(tiles_count, VL, TY // 8, 8, TX // 16, 16) * mask[:, None, :, None, :, None]).reshape(tiles_count, VL, TY, TX)
    weights = jnp.zeros_like(right_side)
    residual = right_side
    direction = right_side
    norm_now = jnp.sum(residual * residual)
    for step in range(ITERS):
        image = apply_operator(direction, perturbations, obs_weight)
        length = norm_now / jnp.sum(direction * image)
        weights = weights + length * direction
        residual = residual - length * image
        if step + 1 < ITERS:
            norm_next = jnp.sum(residual * residual)
            direction = residual + norm_next / norm_now * direction
            norm_now = norm_next
    return (weights, residual)
```

```python
import functools

import jax
import jax.numpy as jnp
import numpy as np
from jax import lax
from jax.experimental import pallas as pl
from jax.experimental.pallas import tpu as pltpu
from jax.sharding import PartitionSpec as P

TY = 16
TX = 256
VL = 6
KL = 16
HALF = 128
HIGH = lax.Precision.HIGHEST


def filter_constants():
    j = np.arange(-8, 9).astype(np.float64)
    taps = (np.exp(-j * j / 32.0) / np.sqrt(np.sum(np.exp(-j * j / 16.0)))).astype(np.float32)

    def tap(offset):
        return np.where(np.abs(offset) <= 8, taps[np.clip(offset + 8, 0, 16)], np.float32(0))

    y = np.arange(TY)
    own = tap(y[None, :] - y[:, None])
    above = tap(np.arange(-8, 0)[None, :] - y[:, None])
    below = tap(np.arange(16, 24)[None, :] - y[:, None])
    eye = np.eye(8, dtype=np.float32)
    rows = np.concatenate([np.kron(eye, own), np.kron(eye, above), np.kron(eye, below)], axis=1)
    strip = np.concatenate([above, own, below], axis=1)
    x = np.arange(TX)
    columns = tap(x[:, None] - x[None, :])
    c = np.arange(8)
    eye16 = np.eye(16, dtype=np.float32)
    left = np.kron(eye16, tap((c[:, None] - 8) - c[None, :]))
    right = np.kron(eye16, tap((c[:, None] + 8) - c[None, :]))
    spread = (np.arange(16)[:, None] == x[None, :] // 16).astype(np.float32)
    return rows, columns, left, right, strip, spread


def dot(a, b):
    return jnp.dot(a, b, precision=HIGH, preferred_element_type=jnp.float32)


def kernel(
    tiles, tcols, mems,
    src_hbm, pert_hbm, prec_hbm, cov_hbm, rows_hbm, columns_hbm, left_hbm, right_hbm, strip_hbm, spread_hbm,
    w_hbm, res_hbm,
    v0, pert, obsw, cov, rows, columns, left, right, strip, spread, strip_l, strip_r,
    fields, outs, above, below, lhalo, rhalo, packs, inc, rsbuf, agbuf, stat, ar1, ar2, ar3,
    load_sem, store_sem, halo_send, halo_recv, rs_send, rs_recv, ag_send, ag_recv, ar_send, ar_recv,
):
    t = lax.axis_index("tile")
    m = lax.axis_index("mem")
    depth = tiles // 4

    def at_tile(offset):
        return {"tile": lax.rem(t + (offset + tiles), tiles), "mem": m}

    def at_mem(offset):
        return {"tile": t, "mem": lax.rem(m + offset, mems)}

    def at_quad(offset):
        q = lax.rem(t, 4)
        return {"tile": t - q + lax.rem(q + offset, 4), "mem": m}

    def at_depth(offset):
        return {"tile": lax.rem(t + 4 * offset, tiles), "mem": m}

    loads = []
    for i, (source, target) in enumerate(
        (
            (src_hbm.at[0], v0), (pert_hbm.at[0], pert), (prec_hbm.at[0], obsw), (cov_hbm.at[0], cov),
            (rows_hbm, rows), (columns_hbm, columns), (left_hbm, left), (right_hbm, right),
            (strip_hbm, strip), (spread_hbm, spread),
        )
    ):
        copy = pltpu.make_async_copy(source, target, load_sem.at[i])
        copy.start()
        loads.append(copy)

    neighbours = (tcols, -tcols, 1, -1, tcols + 1, -tcols - 1, tcols - 1, 1 - tcols)
    barrier = pltpu.get_barrier_semaphore()
    greeted = (
        [at_tile(d) for d in neighbours]
        + [at_mem(d) for d in range(1, mems)]
        + [at_quad(d) for d in range(1, 4)]
        + [at_depth(d) for d in range(1, depth)]
    )
    for device in greeted:
        pl.semaphore_signal(barrier, inc=1, device_id=device, device_id_type=pl.DeviceIdType.MESH)
    pl.semaphore_wait(barrier, len(greeted))

    sends = []

    def remote(source, target, send, recv, device):
        copy = pltpu.make_async_remote_copy(
            src_ref=source, dst_ref=target, send_sem=send, recv_sem=recv,
            device_id=device, device_id_type=pl.DeviceIdType.MESH,
        )
        copy.start()
        sends.append(copy)
        return copy

    lane = lax.broadcasted_iota(jnp.int32, (TY, HALF), 1)

    def send_rows(n, source):
        return [
            remote(source.at[:, pl.ds(8, 8), :], above.at[n], halo_send.at[n, 0], halo_recv.at[n, 0], at_tile(tcols)),
            remote(source.at[:, pl.ds(0, 8), :], below.at[n], halo_send.at[n, 1], halo_recv.at[n, 1], at_tile(-tcols)),
        ]

    def send_edges(n, field):
        packed_l = jnp.zeros((TY, HALF), jnp.float32)
        packed_r = jnp.zeros((TY, HALF), jnp.float32)
        for k in range(KL):
            here = lane // 8 == k
            value_l = field[k, :, 0:HALF]
            value_r = field[k, :, HALF:TX]
            value_l = pltpu.roll(value_l, 8 * k, 1) if k else value_l
            value_r = pltpu.roll(value_r, 8 * k + 8, 1) if k < KL - 1 else value_r
            packed_l = jnp.where(here, value_l, packed_l)
            packed_r = jnp.where(here, value_r, packed_r)
        packs[n, 0] = packed_l
        packs[n, 1] = packed_r
        pl_ref, pr_ref = packs.at[n, 0], packs.at[n, 1]
        lh, rh = lhalo.at[n], rhalo.at[n]
        s, r = halo_send, halo_recv
        top, bottom = pl.ds(0, 8), pl.ds(8, 8)
        return [
            remote(pr_ref, lh.at[pl.ds(8, 16), :], s.at[n, 2], r.at[n, 2], at_tile(1)),
            remote(pl_ref, rh.at[pl.ds(8, 16), :], s.at[n, 3], r.at[n, 3], at_tile(-1)),
            remote(pr_ref.at[bottom, :], lh.at[pl.ds(0, 8), :], s.at[n, 4], r.at[n, 4], at_tile(tcols + 1)),
            remote(pl_ref.at[top, :], rh.at[pl.ds(24, 8), :], s.at[n, 5], r.at[n, 5], at_tile(-tcols - 1)),
            remote(pl_ref.at[bottom, :], rh.at[pl.ds(0, 8), :], s.at[n, 6], r.at[n, 6], at_tile(tcols - 1)),
            remote(pr_ref.at[top, :], lh.at[pl.ds(24, 8), :], s.at[n, 7], r.at[n, 7], at_tile(1 - tcols)),
        ]

    def smooth(n, field, target, copies):
        for copy in copies:
            copy.wait_recv()
        edge_l = dot(dot(strip_l[...], lhalo[n]), left[...])
        edge_r = dot(dot(strip_r[...], rhalo[n]), right[...])
        for group in range(2):
            ks = pl.ds(8 * group, 8)
            stacked = jnp.concatenate(
                [
                    field[ks].reshape(128, TX),
                    above[n, ks].reshape(64, TX),
                    below[n, ks].reshape(64, TX),
                ],
                axis=0,
            )
            filtered = dot(dot(rows[...], stacked), columns[...])
            for i in range(8):
                k = 8 * group + i
                part = filtered[TY * i : TY * i + TY]
                low, high = part[:, :HALF], part[:, HALF:]
                add_l = pltpu.roll(edge_l, HALF - 8 * k, 1) if k else edge_l
                add_r = pltpu.roll(edge_r, 120 - 8 * k, 1) if k < KL - 1 else edge_r
                target[k, :, 0:HALF] = low + jnp.where(lane < 8, add_l, 0.0)
                target[k, :, HALF:TX] = high + jnp.where(lane >= 120, add_r, 0.0)

    def increment(n, field):
        def body(k, totals):
            value = field[k]
            return tuple(totals[v] + pert[k, v].astype(jnp.float32) * value for v in range(VL))

        zero = jnp.zeros((TY, TX), jnp.float32)
        totals = lax.fori_loop(0, KL, body, (zero,) * VL)
        for v in range(VL):
            for h in range(2):
                inc[n, h, pl.ds(v, TY, stride=8), :] = totals[v][:, HALF * h : HALF * h + HALF]
        rows_of = lambda y: pl.ds(pl.multiple_of(8 * y, 8), 8)
        copies = []
        for d in range(1, mems):
            there = lax.rem(m + d, mems)
            for piece in range(TY // mems):
                copies.append(
                    remote(
                        inc.at[n, :, rows_of(there * (TY // mems) + piece), :], rsbuf.at[n, d - 1, piece],
                        rs_send.at[n, d - 1, piece], rs_recv.at[n, d - 1, piece], at_mem(d),
                    )
                )
        for copy in copies:
            copy.wait_recv()
        copies = []
        for piece in range(TY // mems):
            mine = rows_of(m * (TY // mems) + piece)
            total = inc[n, :, mine, :]
            for d in range(1, mems):
                total = total + rsbuf[n, d - 1, piece]
            agbuf[n, :, mine, :] = total
        for d in range(1, mems):
            for piece in range(TY // mems):
                mine = rows_of(m * (TY // mems) + piece)
                copies.append(
                    remote(
                        agbuf.at[n, :, mine, :], agbuf.at[n, :, mine, :],
                        ag_send.at[n, d - 1, piece], ag_recv.at[n, d - 1, piece], at_mem(d),
                    )
                )
        for copy in copies:
            copy.wait_recv()

    def adjoint(n, target):
        weighted = []
        for v in range(VL):
            halves = [agbuf[n, h, pl.ds(v, TY, stride=8), :] for h in range(2)]
            weighted.append(obsw[v] * jnp.concatenate(halves, axis=1))

        def body(k, carry):
            total = pert[k, 0].astype(jnp.float32) * weighted[0]
            for v in range(1, VL):
                total = total + pert[k, v].astype(jnp.float32) * weighted[v]
            target[k] = total
            return carry

        lax.fori_loop(0, KL, body, 0)

    g0, v1, g1, u = fields.at[0], fields.at[1], fields.at[2], fields.at[3]
    v2 = fields.at[4]

    copies = send_rows(0, src_hbm.at[0])
    loads[0].wait()
    copies += send_edges(0, v0)
    for copy in loads[1:]:
        copy.wait()

    def known(position, least, below_that):
        return jnp.logical_and(position >= least, position < below_that).astype(jnp.float32)

    def flags(offset):
        s = lax.rem(t + (offset + tiles), tiles)
        return known(s, tcols, tiles), known(s, 0, tiles - tcols)

    top, bottom = flags(0)
    rows[:, 128:192] = rows[:, 128:192] * top
    rows[:, 192:256] = rows[:, 192:256] * bottom
    column = lax.broadcasted_iota(jnp.int32, (TY, 32), 1)
    for offset, target in ((-1, strip_l), (1, strip_r)):
        top, bottom = flags(offset)
        scale = jnp.where(column < 8, top, jnp.where(column >= 24, bottom, 1.0))
        target[...] = strip[...] * scale
    mask = dot(cov[...].astype(jnp.float32), spread[...])
    mask = jnp.concatenate([jnp.broadcast_to(mask[i : i + 1], (8, TX)) for i in range(2)], axis=0)
    for v in range(VL):
        obsw[v] = obsw[v] * mask
    inc[...] = jnp.zeros_like(inc)

    smooth(0, v0, u, copies)
    increment(0, u)
    adjoint(0, g0)
    copies = send_rows(1, g0)
    copies += send_edges(1, g0)
    smooth(1, g0, v1, copies)
    copies = send_rows(2, v1)
    copies += send_edges(2, v1)
    smooth(2, v1, u, copies)
    increment(1, u)
    adjoint(1, g1)
    copies = send_rows(3, g1)
    copies += send_edges(3, g1)
    smooth(3, g1, v2, copies)

    def gram(k, totals):
        a, b, c = v0[k], v1[k], v2[k]
        terms = (a * a, a * b, b * b, a * c, b * c)
        return tuple(total + term for total, term in zip(totals, terms))

    totals = lax.fori_loop(0, KL, gram, (jnp.zeros((TY, TX), jnp.float32),) * 5)
    lane1 = lax.broadcasted_iota(jnp.int32, (1, HALF), 1)
    row = jnp.zeros((1, HALF), jnp.float32)
    for i, total in enumerate(totals):
        line = jnp.sum(total, axis=0, keepdims=True)
        row = jnp.where(lane1 == i, jnp.sum(line, axis=1, keepdims=True), row)
    base = 0
    for stage, (buffer, count, place) in enumerate(((ar1, 4, at_quad), (ar2, mems, at_mem), (ar3, depth, at_depth))):
        stat[stage] = row
        copies = [
            remote(stat.at[stage], buffer.at[d - 1], ar_send.at[base + d], ar_recv.at[base + d], place(d))
            for d in range(1, count)
        ]
        base += count
        for copy in copies:
            copy.wait_recv()
        for d in range(1, count):
            row = row + buffer[d - 1]

    aa, ab, bb, ac, bc = (
        jnp.sum(jnp.where(lane1 == i, row, 0.0), axis=1, keepdims=True) for i in range(5)
    )
    first = aa / (aa + ab)
    rest = ab / (aa + ab)
    after = rest * rest * aa - 2.0 * rest * first * ab + first * first * bb
    along = rest + after / aa
    curved = along * along * (aa + ab) - along * first * (2.0 * ab + bb + ac) + first * first * (bb + bc)
    second = after / curved
    w0, w1 = first + second * along, -(second * first)
    q0, q1, q2 = rest - second * along, -first - second * (along - first), second * first
    for k in range(KL):
        a, b, c = v0[k], v1[k], v2[k]
        outs[0, k] = w0 * a + w1 * b
        outs[1, k] = q0 * a + q1 * b + q2 * c
    stores = [
        pltpu.make_async_copy(outs.at[i], target.at[0], store_sem.at[i]) for i, target in enumerate((w_hbm, res_hbm))
    ]
    for copy in stores:
        copy.start()
    for copy in sends:
        copy.wait_send()
    for copy in stores:
        copy.wait()


def local(tiles, tcols, mems, right_side, perturbations, precision, covered):
    constants = [jnp.asarray(array) for array in filter_constants()]
    field = jax.ShapeDtypeStruct((1, KL, TY, TX), jnp.float32)
    f32 = jnp.float32
    pieces = TY // mems
    scratch = [
        pltpu.VMEM((KL, TY, TX), f32),
        pltpu.VMEM((KL, VL, TY, TX), jnp.bfloat16),
        pltpu.VMEM((VL, TY, TX), f32),
        pltpu.VMEM((2, 16), jnp.int32),
        pltpu.VMEM((128, 256), f32),
        pltpu.VMEM((256, 256), f32),
        pltpu.VMEM((128, 128), f32),
        pltpu.VMEM((128, 128), f32),
        pltpu.VMEM((16, 32), f32),
        pltpu.VMEM((16, 256), f32),
        pltpu.VMEM((16, 32), f32),
        pltpu.VMEM((16, 32), f32),
        pltpu.VMEM((5, KL, TY, TX), f32),
        pltpu.VMEM((2, KL, TY, TX), f32),
        pltpu.VMEM((4, KL, 8, TX), f32),
        pltpu.VMEM((4, KL, 8, TX), f32),
        pltpu.VMEM((4, 32, HALF), f32),
        pltpu.VMEM((4, 32, HALF), f32),
        pltpu.VMEM((4, 2, TY, HALF), f32),
        pltpu.VMEM((2, 2, 128, HALF), f32),
        pltpu.VMEM((2, mems - 1, pieces, 2, 8, HALF), f32),
        pltpu.VMEM((2, 2, 128, HALF), f32),
        pltpu.VMEM((3, 1, HALF), f32),
        pltpu.VMEM((3, 1, HALF), f32),
        pltpu.VMEM((mems - 1, 1, HALF), f32),
        pltpu.VMEM((tiles // 4 - 1, 1, HALF), f32),
        pltpu.SemaphoreType.DMA((10,)),
        pltpu.SemaphoreType.DMA((2,)),
        pltpu.SemaphoreType.DMA((4, 8)),
        pltpu.SemaphoreType.DMA((4, 8)),
        pltpu.SemaphoreType.DMA((2, mems - 1, pieces)),
        pltpu.SemaphoreType.DMA((2, mems - 1, pieces)),
        pltpu.SemaphoreType.DMA((2, mems - 1, pieces)),
        pltpu.SemaphoreType.DMA((2, mems - 1, pieces)),
        pltpu.SemaphoreType.DMA((4 + mems + tiles // 4,)),
        pltpu.SemaphoreType.DMA((4 + mems + tiles // 4,)),
    ]
    return pl.pallas_call(
        functools.partial(kernel, tiles, tcols, mems),
        out_shape=(field, field),
        in_specs=[pl.BlockSpec(memory_space=pl.ANY)] * 10,
        out_specs=(pl.BlockSpec(memory_space=pl.ANY),) * 2,
        scratch_shapes=scratch,
        compiler_params=pltpu.CompilerParams(
            collective_id=0, has_side_effects=True, vmem_limit_bytes=40 * 2**20
        ),
        name="conjugate_gradients",
    )(right_side, perturbations, precision, covered, *constants)


def solution(mesh, tcols=8):
    in_specs = (
        P("tile", "mem", None, None),
        P("tile", "mem", None, None, None),
        P("tile", None, None, None),
        P("tile", None, None),
    )
    out_specs = (P("tile", "mem", None, None),) * 2
    body = functools.partial(local, mesh.shape["tile"], tcols, mesh.shape["mem"])
    return jax.shard_map(body, mesh=mesh, in_specs=in_specs, out_specs=out_specs, check_vma=False)
```

```python
import functools

import jax
import jax.numpy as jnp
import numpy as np
from jax import lax
from jax.experimental import pallas as pl
from jax.experimental.pallas import tpu as pltpu
from jax.sharding import PartitionSpec as P

TY = 16
TX = 256
VL = 6
KL = 16
HALF = 128
GROUPS = 2
KG = KL // GROUPS
F32 = jnp.float32
BF16 = jnp.bfloat16


def three(matrix, dim):
    high = matrix.astype(BF16)
    low = (matrix - high.astype(np.float32)).astype(BF16)
    return np.concatenate([high, low, high] if dim else [high, high, low], axis=dim)


def filter_constants():
    j = np.arange(-8, 9).astype(np.float64)
    taps = (np.exp(-j * j / 32.0) / np.sqrt(np.sum(np.exp(-j * j / 16.0)))).astype(np.float32)

    def tap(offset):
        return np.where(np.abs(offset) <= 8, taps[np.clip(offset + 8, 0, 16)], np.float32(0))

    y = np.arange(TY)
    own = tap(y[None, :] - y[:, None])
    above = tap(np.arange(-8, 0)[None, :] - y[:, None])
    below = tap(np.arange(16, 24)[None, :] - y[:, None])
    eye = np.eye(KG, dtype=np.float32)
    rows = np.concatenate(
        [three(np.kron(eye, own), 1), three(np.concatenate([np.kron(eye, above), np.kron(eye, below)], axis=1), 1)], axis=1
    )
    strip = three(np.concatenate([above, own, below], axis=1), 1)
    x = np.arange(TX)
    columns = three(tap(x[:, None] - x[None, :]), 0)
    c = np.arange(8)
    eye16 = np.eye(16, dtype=np.float32)
    none = np.zeros((HALF, HALF), np.float32)
    left = np.kron(eye16, tap((c[:, None] - 8) - c[None, :]))
    right = np.kron(eye16, tap((c[:, None] + 8) - c[None, :]))
    edges = three(np.block([[left, none], [none, right]]), 0)
    spread = (np.arange(16)[:, None] == x[None, :] // 16).astype(np.float32)
    return rows, columns, edges, strip, spread


def split(value):
    high = value.astype(BF16)
    return high, (value - high.astype(F32)).astype(BF16)


def left_product(constant, value):
    high, low = split(value)
    return jnp.dot(constant, jnp.concatenate([high, high, low], axis=0), preferred_element_type=F32)


def right_product(value, constant):
    high, low = split(value)
    return jnp.dot(jnp.concatenate([high, low, high], axis=1), constant, preferred_element_type=F32)


def kernel(
    tiles, tcols, mems,
    src_hbm, pert_hbm, prec_hbm, cov_hbm, rows_hbm, columns_hbm, edges_hbm, strip_hbm, spread_hbm,
    w_out, r_out,
    v0, pert, obsw, cov, rows, columns, edges, strip, spread, fmask, tmask,
    fields, above, below, ehalo, packs, inc, rsbuf, agbuf, stat, ar1, ar2,
    load_sem, halo_send, halo_recv, rs_send, rs_recv, ag_send, ag_recv, ar_send, ar_recv,
):
    t = lax.axis_index("tile")
    m = lax.axis_index("mem")
    depth = tiles // 4

    def at_tile(offset):
        return {"tile": lax.rem(t + (offset + tiles), tiles), "mem": m}

    def at_mem(offset):
        return {"tile": t, "mem": lax.rem(m + offset, mems)}

    def at_plane(offset):
        q = lax.rem(t, 4)
        return {"tile": t - q + lax.rem(q + offset // mems, 4), "mem": lax.rem(m + offset % mems, mems)}

    def at_depth(offset):
        return {"tile": lax.rem(t + 4 * offset, tiles), "mem": m}

    neighbours = (tcols, -tcols, 1, -1, tcols + 1, -tcols - 1, tcols - 1, 1 - tcols)
    barrier = pltpu.get_barrier_semaphore()
    greeted = [at_tile(d) for d in neighbours] + [at_mem(d) for d in range(1, mems)]
    for device in greeted:
        pl.semaphore_signal(barrier, inc=1, device_id=device, device_id_type=pl.DeviceIdType.MESH)

    loads = []
    for i, (source, target) in enumerate(
        (
            (src_hbm.at[0], v0), (pert_hbm.at[0], pert), (prec_hbm.at[0], obsw), (cov_hbm.at[0], cov),
            (rows_hbm, rows), (columns_hbm, columns), (edges_hbm, edges), (strip_hbm, strip), (spread_hbm, spread),
        )
    ):
        copy = pltpu.make_async_copy(source, target, load_sem.at[i])
        copy.start()
        loads.append(copy)
    pl.semaphore_wait(barrier, len(greeted))

    sends = []

    def remote(source, target, send, recv, device):
        copy = pltpu.make_async_remote_copy(
            src_ref=source, dst_ref=target, send_sem=send, recv_sem=recv,
            device_id=device, device_id_type=pl.DeviceIdType.MESH,
        )
        copy.start()
        sends.append(copy)
        return copy

    lane = lax.broadcasted_iota(jnp.int32, (TY, HALF), 1)
    arrivals = [[[] for g in range(GROUPS)] for n in range(4)]

    def members(g):
        return pl.ds(KG * g, KG)

    def send_rows(n, g, source):
        s, r = halo_send.at[n, g], halo_recv.at[n, g]
        arrivals[n][g] += [
            remote(source.at[members(g), pl.ds(8, 8), :], above.at[n, g], s.at[0], r.at[0], at_tile(tcols)),
            remote(source.at[members(g), pl.ds(0, 8), :], below.at[n, g], s.at[1], r.at[1], at_tile(-tcols)),
        ]

    def send_edges(n, g, field):
        packed_l = jnp.zeros((TY, HALF), F32)
        packed_r = jnp.zeros((TY, HALF), F32)
        for i in range(KG):
            here = lane // 8 == i
            value_l = field[KG * g + i, :, 0:HALF]
            value_l = pltpu.roll(value_l, 8 * i, 1) if i else value_l
            value_r = pltpu.roll(field[KG * g + i, :, HALF:TX], 8 * i + 8, 1)
            packed_l = jnp.where(here, value_l, packed_l)
            packed_r = jnp.where(here, value_r, packed_r)
        packs[n, g, :, 0:HALF] = packed_l
        packs[n, g, :, HALF:TX] = packed_r
        left, right = pl.ds(0, HALF), pl.ds(HALF, HALF)
        top, bottom, whole = pl.ds(0, 8), pl.ds(8, 8), pl.ds(0, TY)
        for i, (rows_sent, side, place, half, offset) in enumerate(
            (
                (bottom, right, 0, left, tcols + 1), (top, left, 24, right, -tcols - 1),
                (bottom, left, 0, right, tcols - 1), (top, right, 24, left, 1 - tcols),
                (whole, right, 8, left, 1), (whole, left, 8, right, -1),
            )
        ):
            height = TY if place == 8 else 8
            arrivals[n][g].append(
                remote(
                    packs.at[n, g, rows_sent, side], ehalo.at[n, g, pl.ds(place, height), half],
                    halo_send.at[n, g, 2 + i], halo_recv.at[n, g, 2 + i], at_tile(offset),
                )
            )

    def flags(offset):
        s = lax.rem(t + (offset + tiles), tiles)
        return (s >= tcols).astype(F32), (s < tiles - tcols).astype(F32)

    here_top, here_bottom = flags(0)

    def smooth(n, g, field, target):
        partial = left_product(rows[:, : 3 * HALF], field[members(g)].reshape(KG * TY, TX))
        for copy in arrivals[n][g]:
            copy.wait_recv()
        edge = right_product(left_product(strip[...], ehalo[n, g] * fmask[...]), edges[...])
        halo = jnp.concatenate(
            [above[n, g].reshape(KG * 8, TX) * here_top, below[n, g].reshape(KG * 8, TX) * here_bottom], axis=0
        )
        filtered = right_product(partial + left_product(rows[:, 3 * HALF :], halo), columns[...])
        edge_l, edge_r = edge[:, :HALF], edge[:, HALF:]
        for i in range(KG):
            k = KG * g + i
            part = filtered[TY * i : TY * i + TY]
            add_l = pltpu.roll(edge_l, HALF - 8 * i, 1) if i else edge_l
            add_r = pltpu.roll(edge_r, 120 - 8 * i, 1)
            target[k, :, 0:HALF] = part[:, :HALF] + jnp.where(lane < 8, add_l, 0.0)
            target[k, :, HALF:TX] = part[:, HALF:] + jnp.where(lane >= 120, add_r, 0.0)

    def corners(n, g):
        return right_product(left_product(strip[...], ehalo[n, g] * tmask[...]), edges[...])

    def gathered(field, g, totals):
        def body(k, totals):
            value = field[k]
            return tuple(totals[v] + pert[k, v].astype(F32) * value for v in range(VL))

        return lax.fori_loop(KG * g, KG * g + KG, body, totals)

    pieces = TY // mems

    def rows_of(y):
        return pl.ds(pl.multiple_of(8 * y, 8), 8)

    def exchange(n, totals, meanwhile):
        for v in range(VL):
            for h in range(2):
                inc[n, h, pl.ds(v, TY, stride=8), :] = totals[v][:, HALF * h : HALF * h + HALF]
        copies = []
        for d in range(1, mems):
            there = lax.rem(m + d, mems)
            for piece in range(pieces):
                copies.append(
                    remote(
                        inc.at[n, :, rows_of(there * pieces + piece), :], rsbuf.at[n, d - 1, piece],
                        rs_send.at[n, d - 1, piece], rs_recv.at[n, d - 1, piece], at_mem(d),
                    )
                )
        result = meanwhile()
        for copy in copies:
            copy.wait_recv()
        copies = []
        for piece in range(pieces):
            mine = rows_of(m * pieces + piece)
            total = inc[n, :, mine, :]
            for d in range(1, mems):
                total = total + rsbuf[n, d - 1, piece]
            agbuf[n, :, mine, :] = total
        for d in range(1, mems):
            for piece in range(pieces):
                mine = rows_of(m * pieces + piece)
                copies.append(
                    remote(
                        agbuf.at[n, :, mine, :], agbuf.at[n, :, mine, :],
                        ag_send.at[n, d - 1, piece], ag_recv.at[n, d - 1, piece], at_mem(d),
                    )
                )
        for copy in copies:
            copy.wait_recv()
        return result

    def weighted(n):
        values = []
        for v in range(VL):
            halves = [agbuf[n, h, pl.ds(v, TY, stride=8), :] for h in range(2)]
            values.append(obsw[v] * jnp.concatenate(halves, axis=1))
        return values

    def adjoint(g, values, target):
        def body(k, carry):
            total = pert[k, 0].astype(F32) * values[0]
            for v in range(1, VL):
                total = total + pert[k, v].astype(F32) * values[v]
            target[k] = total
            return carry

        lax.fori_loop(KG * g, KG * g + KG, body, 0)

    g0, g1, u0, u1, v1, v2 = (fields.at[i] for i in range(6))
    zeros = (jnp.zeros((TY, TX), F32),) * VL

    send_rows(0, 0, src_hbm.at[0])
    loads[0].wait()
    for g in range(GROUPS):
        send_edges(0, g, v0)
    for g in range(1, GROUPS):
        send_rows(0, g, src_hbm.at[0])
    for copy in loads[1:]:
        copy.wait()
    row8 = lax.broadcasted_iota(jnp.int32, (32, TX), 0)
    is_left = lax.broadcasted_iota(jnp.int32, (32, TX), 1) < HALF

    def masked(top, bottom):
        return jnp.where(row8 < 8, top, jnp.where(row8 >= 24, bottom, 1.0))

    mask = jnp.where(is_left, masked(*flags(-1)), masked(*flags(1)))
    fmask[...] = mask
    tmask[...] = masked(here_top, here_bottom) - mask
    mask = jnp.dot(cov[...].astype(F32), spread[...], preferred_element_type=F32)
    mask = jnp.concatenate([jnp.broadcast_to(mask[i : i + 1], (8, TX)) for i in range(2)], axis=0)
    for v in range(VL):
        obsw[v] = obsw[v] * mask
    inc[...] = jnp.zeros_like(inc)

    totals = zeros
    for g in range(GROUPS):
        smooth(0, g, v0, u0)
        totals = gathered(u0, g, totals)
    twist_0 = exchange(0, totals, lambda: [corners(0, g) for g in range(GROUPS)])
    values = weighted(0)
    for g in range(GROUPS):
        adjoint(g, values, g0)
        send_edges(1, g, g0)
        send_rows(1, g, g0)
    for g in range(GROUPS):
        smooth(1, g, g0, v1)
        send_edges(2, g, v1)
        send_rows(2, g, v1)
    totals = zeros
    for g in range(GROUPS):
        smooth(2, g, v1, u1)
        totals = gathered(u1, g, totals)

    def lines(totals):
        return [jnp.sum(total[:, :HALF] + total[:, HALF:], axis=0, keepdims=True) for total in totals]

    def known_products():
        def body(k, totals):
            a, b = v0[k], v1[k]
            return totals[0] + a * a, totals[1] + a * b, totals[2] + b * b

        return [corners(2, g) for g in range(GROUPS)], lines(lax.fori_loop(0, KL, body, zeros[:3]))

    twist_1, sums = exchange(1, totals, known_products)
    values = weighted(1)
    for g in range(GROUPS):
        adjoint(g, values, g1)
        send_edges(3, g, g1)
        send_rows(3, g, g1)

    def new_products(k, totals):
        return totals[0] + u0[k] * g1[k], totals[1] + u1[k] * g1[k]

    totals = lax.fori_loop(0, KL, new_products, zeros[:2])
    totals = [
        total + sum(twist[g] * packs[3, g] for g in range(GROUPS)) for total, twist in zip(totals, (twist_0, twist_1))
    ]
    sums = sums + lines(totals)
    lane1 = lax.broadcasted_iota(jnp.int32, (1, HALF), 1)
    row = jnp.zeros((1, HALF), F32)
    for i, line in enumerate(sums):
        row = jnp.where(lane1 == i, jnp.sum(line, axis=1, keepdims=True), row)

    def share(stage, buffer, count, place, base):
        stat[stage] = row
        return [
            remote(stat.at[stage], buffer.at[d - 1], ar_send.at[base + d], ar_recv.at[base + d], place(d))
            for d in range(1, count)
        ]

    def collect(buffer, waited):
        for copy in waited:
            copy.wait_recv()
        return row + jnp.sum(buffer[...], axis=0)

    shared = share(0, ar1, 4 * mems, at_plane, 0)
    for g in range(GROUPS - 1):
        smooth(3, g, g1, v2)
    row = collect(ar1, shared)
    shared = share(1, ar2, depth, at_depth, 4 * mems)
    smooth(3, GROUPS - 1, g1, v2)
    row = collect(ar2, shared)

    aa, ab, bb, ac, bc = (
        jnp.sum(jnp.where(lane1 == i, row, 0.0), axis=1, keepdims=True) for i in range(5)
    )
    first = aa / (aa + ab)
    rest = ab / (aa + ab)
    after = rest * rest * aa - 2.0 * rest * first * ab + first * first * bb
    along = rest + after / aa
    curved = along * along * (aa + ab) - along * first * (2.0 * ab + bb + ac) + first * first * (bb + bc)
    second = after / curved
    w0, w1 = first + second * along, -(second * first)
    q0, q1, q2 = rest - second * along, -first - second * (along - first), second * first
    for k in range(KL):
        a, b, c = v0[k], v1[k], v2[k]
        w_out[0, k] = w0 * a + w1 * b
        r_out[0, k] = q0 * a + q1 * b + q2 * c
    for copy in sends:
        copy.wait_send()


def local(tiles, tcols, mems, right_side, perturbations, precision, covered):
    constants = [jnp.asarray(array) for array in filter_constants()]
    field = jax.ShapeDtypeStruct((1, KL, TY, TX), jnp.float32)
    f32 = jnp.float32
    pieces = TY // mems
    scratch = [
        pltpu.VMEM((KL, TY, TX), f32),
        pltpu.VMEM((KL, VL, TY, TX), BF16),
        pltpu.VMEM((VL, TY, TX), f32),
        pltpu.VMEM((2, 16), jnp.int32),
        *[pltpu.VMEM(array.shape, array.dtype) for array in constants],
        pltpu.VMEM((32, TX), f32),
        pltpu.VMEM((32, TX), f32),
        pltpu.VMEM((6, KL, TY, TX), f32),
        pltpu.VMEM((4, GROUPS, KG, 8, TX), f32),
        pltpu.VMEM((4, GROUPS, KG, 8, TX), f32),
        pltpu.VMEM((4, GROUPS, 32, TX), f32),
        pltpu.VMEM((4, GROUPS, TY, TX), f32),
        pltpu.VMEM((2, 2, 128, HALF), f32),
        pltpu.VMEM((2, mems - 1, pieces, 2, 8, HALF), f32),
        pltpu.VMEM((2, 2, 128, HALF), f32),
        pltpu.VMEM((2, 1, HALF), f32),
        pltpu.VMEM((4 * mems - 1, 1, HALF), f32),
        pltpu.VMEM((tiles // 4 - 1, 1, HALF), f32),
        pltpu.SemaphoreType.DMA((9,)),
        pltpu.SemaphoreType.DMA((4, GROUPS, 8)),
        pltpu.SemaphoreType.DMA((4, GROUPS, 8)),
        pltpu.SemaphoreType.DMA((2, mems - 1, pieces)),
        pltpu.SemaphoreType.DMA((2, mems - 1, pieces)),
        pltpu.SemaphoreType.DMA((2, mems - 1, pieces)),
        pltpu.SemaphoreType.DMA((2, mems - 1, pieces)),
        pltpu.SemaphoreType.DMA((4 * mems + tiles // 4,)),
        pltpu.SemaphoreType.DMA((4 * mems + tiles // 4,)),
    ]
    return pl.pallas_call(
        functools.partial(kernel, tiles, tcols, mems),
        out_shape=(field, field),
        in_specs=[pl.BlockSpec(memory_space=pltpu.MemorySpace.HBM)] * 9,
        out_specs=(pl.BlockSpec(memory_space=pltpu.MemorySpace.VMEM),) * 2,
        scratch_shapes=scratch,
        compiler_params=pltpu.CompilerParams(
            collective_id=0, has_side_effects=True, vmem_limit_bytes=40 * 2**20
        ),
        name="conjugate_gradients",
    )(*[pltpu.with_memory_space_constraint(x, pltpu.MemorySpace.HBM) for x in (right_side, perturbations, precision, covered, *constants)])


def solution(mesh, tcols=8):
    in_specs = (
        P("tile", "mem", None, None),
        P("tile", "mem", None, None, None),
        P("tile", None, None, None),
        P("tile", None, None),
    )
    out_specs = (P("tile", "mem", None, None),) * 2
    body = functools.partial(local, mesh.shape["tile"], tcols, mesh.shape["mem"])
    return jax.shard_map(body, mesh=mesh, in_specs=in_specs, out_specs=out_specs, check_vma=False)
```

```python
import functools

import jax
import jax.numpy as jnp
import numpy as np
from jax import lax
from jax.experimental import pallas as pl
from jax.experimental.pallas import tpu as pltpu
from jax.sharding import PartitionSpec as P

TY = 16
TX = 256
VL = 6
KL = 16
HALF = 128
GROUPS = 2
KG = KL // GROUPS
F32 = jnp.float32
BF16 = jnp.bfloat16


def three(matrix, dim):
    high = matrix.astype(BF16)
    low = (matrix - high.astype(np.float32)).astype(BF16)
    return np.concatenate([high, low, high] if dim else [high, high, low], axis=dim)


def filter_constants():
    j = np.arange(-8, 9).astype(np.float64)
    taps = (np.exp(-j * j / 32.0) / np.sqrt(np.sum(np.exp(-j * j / 16.0)))).astype(np.float32)

    def tap(offset):
        return np.where(np.abs(offset) <= 8, taps[np.clip(offset + 8, 0, 16)], np.float32(0))

    y = np.arange(TY)
    own = tap(y[None, :] - y[:, None])
    above = tap(np.arange(-8, 0)[None, :] - y[:, None])
    below = tap(np.arange(16, 24)[None, :] - y[:, None])
    eye = np.eye(KG, dtype=np.float32)
    rows = np.concatenate(
        [three(np.kron(eye, own), 1), three(np.concatenate([np.kron(eye, above), np.kron(eye, below)], axis=1), 1)], axis=1
    )
    strip = three(np.concatenate([above, own, below], axis=1), 1)
    x = np.arange(TX)
    columns = three(tap(x[:, None] - x[None, :]), 0)
    c = np.arange(8)
    eye16 = np.eye(16, dtype=np.float32)
    none = np.zeros((HALF, HALF), np.float32)
    left = np.kron(eye16, tap((c[:, None] - 8) - c[None, :]))
    right = np.kron(eye16, tap((c[:, None] + 8) - c[None, :]))
    edges = three(np.block([[left, none], [none, right]]), 0)
    spread = (np.arange(16)[:, None] == x[None, :] // 16).astype(np.float32)
    return rows, columns, edges, strip, spread


def split(value):
    high = value.astype(BF16)
    return high, (value - high.astype(F32)).astype(BF16)


def left_product(constant, value):
    high, low = split(value)
    return jnp.dot(constant, jnp.concatenate([high, high, low], axis=0), preferred_element_type=F32)


def right_product(value, constant):
    high, low = split(value)
    return jnp.dot(jnp.concatenate([high, low, high], axis=1), constant, preferred_element_type=F32)


def kernel(
    tiles, tcols, mems,
    src_hbm, pert_hbm, prec_hbm, cov_hbm, rows_hbm, columns_hbm, edges_hbm, strip_hbm, spread_hbm,
    w_out, r_out,
    v0, pert, obsw, cov, rows, columns, edges, strip, spread, fmask, tmask,
    fields, rhalo, ehalo, packs, inc, rsbuf, agbuf, wrows, dinc, dbuf, stat, ar1, ar2,
    load_sem, send_sem, rows_recv, edges_recv, rs_recv, ag_recv, d_recv, ar_recv,
):
    t = lax.axis_index("tile")
    m = lax.axis_index("mem")
    depth = tiles // 4

    def at_tile(offset):
        return {"tile": lax.rem(t + (offset + tiles), tiles), "mem": m}

    def at_mem(offset):
        return {"tile": t, "mem": lax.rem(m + offset, mems)}

    def at_plane(offset):
        q = lax.rem(t, 4)
        return {"tile": t - q + lax.rem(q + offset // mems, 4), "mem": lax.rem(m + offset % mems, mems)}

    def at_depth(offset):
        return {"tile": lax.rem(t + 4 * offset, tiles), "mem": m}

    neighbours = (tcols, -tcols, 1, -1, tcols + 1, -tcols - 1, tcols - 1, 1 - tcols)
    barrier = pltpu.get_barrier_semaphore()
    greeted = [at_tile(d) for d in neighbours] + [at_mem(d) for d in range(1, mems)]
    for device in greeted:
        pl.semaphore_signal(barrier, inc=1, device_id=device, device_id_type=pl.DeviceIdType.MESH)

    loads = []
    for i, (source, target) in enumerate(
        (
            (src_hbm.at[0], v0), (pert_hbm.at[0], pert), (prec_hbm.at[0], obsw), (cov_hbm.at[0], cov),
            (rows_hbm, rows), (columns_hbm, columns), (edges_hbm, edges), (strip_hbm, strip), (spread_hbm, spread),
        )
    ):
        copy = pltpu.make_async_copy(source, target, load_sem.at[i])
        copy.start()
        loads.append(copy)

    def remote(source, target, kind, recv, device):
        pltpu.make_async_remote_copy(
            src_ref=source, dst_ref=target, send_sem=send_sem.at[kind], recv_sem=recv,
            device_id=device, device_id_type=pl.DeviceIdType.MESH,
        ).start()

    def wait_for(buffer, semaphore):
        pltpu.make_async_copy(buffer, buffer, semaphore).wait()

    lane = lax.broadcasted_iota(jnp.int32, (TY, HALF), 1)

    def members(g):
        return pl.ds(KG * g, KG)

    def send_rows(n, g, source):
        remote(source.at[members(g), pl.ds(8, 8), :], rhalo.at[n, g, 0], 0, rows_recv.at[n, g], at_tile(tcols))
        remote(source.at[members(g), pl.ds(0, 8), :], rhalo.at[n, g, 1], 0, rows_recv.at[n, g], at_tile(-tcols))

    def pack_edges(n, g, field):
        packed_l = jnp.zeros((TY, HALF), F32)
        packed_r = jnp.zeros((TY, HALF), F32)
        for i in range(KG):
            here = lane // 8 == i
            value_l = field[KG * g + i, :, 0:HALF]
            value_l = pltpu.roll(value_l, 8 * i, 1) if i else value_l
            value_r = pltpu.roll(field[KG * g + i, :, HALF:TX], 8 * i + 8, 1)
            packed_l = jnp.where(here, value_l, packed_l)
            packed_r = jnp.where(here, value_r, packed_r)
        packs[n, g, :, 0:HALF] = packed_l
        packs[n, g, :, HALF:TX] = packed_r

    def send_edges(n, g):
        left, right = pl.ds(0, HALF), pl.ds(HALF, HALF)
        top, bottom, whole = pl.ds(0, 8), pl.ds(8, 8), pl.ds(0, TY)
        for rows_sent, side, place, half, offset in (
            (bottom, right, 0, left, tcols + 1), (top, left, 24, right, -tcols - 1),
            (bottom, left, 0, right, tcols - 1), (top, right, 24, left, 1 - tcols),
            (whole, right, 8, left, 1), (whole, left, 8, right, -1),
        ):
            height = TY if place == 8 else 8
            remote(
                packs.at[n, g, rows_sent, side], ehalo.at[n, g, pl.ds(place, height), half],
                1, edges_recv.at[n, g], at_tile(offset),
            )

    def flags(offset):
        s = lax.rem(t + (offset + tiles), tiles)
        return (s >= tcols).astype(F32), (s < tiles - tcols).astype(F32)

    here_top, here_bottom = flags(0)

    def smooth(n, g, field, target):
        partial = left_product(rows[:, : 3 * HALF], field[members(g)].reshape(KG * TY, TX))
        wait_for(ehalo.at[n, g], edges_recv.at[n, g])
        edge = right_product(left_product(strip[...], ehalo[n, g] * fmask[...]), edges[...])
        wait_for(rhalo.at[n, g], rows_recv.at[n, g])
        halo = jnp.concatenate(
            [rhalo[n, g, 0].reshape(KG * 8, TX) * here_top, rhalo[n, g, 1].reshape(KG * 8, TX) * here_bottom], axis=0
        )
        filtered = right_product(partial + left_product(rows[:, 3 * HALF :], halo), columns[...])
        edge_l, edge_r = edge[:, :HALF], edge[:, HALF:]
        for i in range(KG):
            k = KG * g + i
            part = filtered[TY * i : TY * i + TY]
            add_l = pltpu.roll(edge_l, HALF - 8 * i, 1) if i else edge_l
            add_r = pltpu.roll(edge_r, 120 - 8 * i, 1)
            target[k, :, 0:HALF] = part[:, :HALF] + jnp.where(lane < 8, add_l, 0.0)
            target[k, :, HALF:TX] = part[:, HALF:] + jnp.where(lane >= 120, add_r, 0.0)

    def corners(n, g):
        return right_product(left_product(strip[...], ehalo[n, g] * tmask[...]), edges[...])

    def gathered(field, g, totals):
        def body(k, totals):
            value = field[k]
            return tuple(totals[v] + pert[k, v].astype(F32) * value for v in range(VL))

        return lax.fori_loop(KG * g, KG * g + KG, body, totals)

    pieces = TY // mems

    def rows_of(y):
        return pl.ds(pl.multiple_of(8 * y, 8), 8)

    def send_corners(n, twist):
        def body(i, totals):
            for g in range(GROUPS):
                k = KG * g + i
                turn = lax.rem(HALF - 8 * i, HALF)
                add_l = jnp.where(lane < 8, pltpu.roll(twist[g][:, :HALF], turn, 1), 0.0)
                add_r = jnp.where(lane >= 120, pltpu.roll(twist[g][:, HALF:], 120 - 8 * i, 1), 0.0)
                totals = tuple(
                    totals[v]
                    + pert[k, v, :, 0:HALF].astype(F32) * add_l
                    + pert[k, v, :, HALF:TX].astype(F32) * add_r
                    for v in range(VL)
                )
            return totals

        totals = lax.fori_loop(0, KG, body, (jnp.zeros((TY, HALF), F32),) * VL)
        for v in range(VL):
            dinc[n, pl.ds(v, TY, stride=8), :] = totals[v]
        for d in range(1, mems):
            for piece in range(pieces):
                remote(
                    dinc.at[n, rows_of(lax.rem(m + d, mems) * pieces + piece), :], dbuf.at[n, d - 1, piece],
                    4, d_recv.at[n], at_mem(d),
                )

    def exchange(n, totals, meanwhile, ready):
        for v in range(VL):
            for h in range(2):
                inc[n, h, pl.ds(v, TY, stride=8), :] = totals[v][:, HALF * h : HALF * h + HALF]
        for d in range(1, mems):
            there = lax.rem(m + d, mems)
            for piece in range(pieces):
                remote(
                    inc.at[n, :, rows_of(there * pieces + piece), :], rsbuf.at[n, d - 1, piece],
                    2, rs_recv.at[n], at_mem(d),
                )
        result = meanwhile()
        wait_for(rsbuf.at[n], rs_recv.at[n])
        for piece in range(pieces):
            mine = rows_of(m * pieces + piece)
            total = inc[n, :, mine, :]
            for d in range(1, mems):
                total = total + rsbuf[n, d - 1, piece]
            agbuf[n, :, mine, :] = total
        for d in range(1, mems):
            for piece in range(pieces):
                mine = rows_of(m * pieces + piece)
                remote(agbuf.at[n, :, mine, :], agbuf.at[n, :, mine, :], 3, ag_recv.at[n], at_mem(d))
        result = ready(result)
        wait_for(rsbuf.at[n], ag_recv.at[n])
        return result

    def weighted(n):
        values = []
        for v in range(VL):
            halves = [agbuf[n, h, pl.ds(v, TY, stride=8), :] for h in range(2)]
            values.append(obsw[v] * jnp.concatenate(halves, axis=1))
        return values

    def adjoint(g, values, target):
        def body(k, carry):
            total = pert[k, 0].astype(F32) * values[0]
            for v in range(1, VL):
                total = total + pert[k, v].astype(F32) * values[v]
            target[k] = total
            return carry

        lax.fori_loop(KG * g, KG * g + KG, body, 0)

    g0, g1, u0, u1, v1, v2 = (fields.at[i] for i in range(6))
    zeros = (jnp.zeros((TY, TX), F32),) * VL

    loads[0].wait()
    for g in range(GROUPS):
        pack_edges(0, g, v0)
    for copy in loads[1:]:
        copy.wait()
    row8 = lax.broadcasted_iota(jnp.int32, (32, TX), 0)
    is_left = lax.broadcasted_iota(jnp.int32, (32, TX), 1) < HALF

    def masked(top, bottom):
        return jnp.where(row8 < 8, top, jnp.where(row8 >= 24, bottom, 1.0))

    mask = jnp.where(is_left, masked(*flags(-1)), masked(*flags(1)))
    fmask[...] = mask
    tmask[...] = masked(here_top, here_bottom) - mask
    for buffer in (inc, wrows, dinc):
        buffer[...] = jnp.zeros_like(buffer)
    mask = jnp.dot(cov[...].astype(F32), spread[...], preferred_element_type=F32)
    mask = jnp.concatenate([jnp.broadcast_to(mask[i : i + 1], (8, TX)) for i in range(2)], axis=0)
    for v in range(VL):
        obsw[v] = obsw[v] * mask
        for h in range(2):
            wrows[h, pl.ds(v, TY, stride=8), :] = obsw[v, :, HALF * h : HALF * h + HALF]

    pl.semaphore_wait(barrier, len(greeted))
    for g in range(GROUPS):
        send_edges(0, g)
    for g in range(GROUPS):
        send_rows(0, g, src_hbm.at[0])
    totals = zeros
    for g in range(GROUPS):
        smooth(0, g, v0, u0)
        totals = gathered(u0, g, totals)
    def corner_sums(n):
        send_corners(n, [corners(2 * n, g) for g in range(GROUPS)])

    exchange(0, totals, lambda: corner_sums(0), lambda result: None)
    values = weighted(0)
    for g in range(GROUPS):
        adjoint(g, values, g0)
        pack_edges(1, g, g0)
        send_edges(1, g)
        send_rows(1, g, g0)
    for g in range(GROUPS):
        smooth(1, g, g0, v1)
        pack_edges(2, g, v1)
        send_edges(2, g)
        send_rows(2, g, v1)
    totals = zeros
    for g in range(GROUPS):
        smooth(2, g, v1, u1)
        totals = gathered(u1, g, totals)

    def lines(totals):
        return [jnp.sum(total[:, :HALF] + total[:, HALF:], axis=0, keepdims=True) for total in totals]

    def known_products():
        def body(k, totals):
            a, b = v0[k], v1[k]
            return totals[0] + a * a, totals[1] + a * b, totals[2] + b * b

        corner_sums(1)
        return lines(lax.fori_loop(0, KL, body, zeros[:3]))

    lane1 = lax.broadcasted_iota(jnp.int32, (1, HALF), 1)

    def share(stage, row, buffer, count, place):
        stat[stage] = row
        for d in range(1, count):
            remote(stat.at[stage], buffer.at[d - 1], 5 + stage, ar_recv.at[stage], place(d))
        return row

    def collect(stage, buffer, row):
        wait_for(buffer, ar_recv.at[stage])
        return row + jnp.sum(buffer[...], axis=0)

    def start_sum(sums):
        for n in range(2):
            wait_for(dbuf.at[n], d_recv.at[n])
        crossed = [jnp.zeros((8, HALF), F32)] * 2
        lane8 = lax.broadcasted_iota(jnp.int32, (8, HALF), 1)
        for piece in range(pieces):
            mine = rows_of(m * pieces + piece)
            value = [wrows[h, mine, :] * agbuf[1, h, mine, :] for h in range(2)]
            outer = jnp.where(lane8 < 8, value[0], jnp.where(lane8 >= 120, value[1], 0.0))
            for n in range(2):
                corner = dinc[n, mine, :]
                for d in range(1, mems):
                    corner = corner + dbuf[n, d - 1, piece]
                crossed[n] = crossed[n] + (
                    agbuf[n, 0, mine, :] * value[0] + agbuf[n, 1, mine, :] * value[1] + corner * outer
                )
        row = jnp.zeros((1, HALF), F32)
        for i, line in enumerate(sums + [jnp.sum(total, axis=0, keepdims=True) for total in crossed]):
            row = jnp.where(lane1 == i, jnp.sum(line, axis=1, keepdims=True), row)
        return share(0, row, ar2, depth, at_depth)

    shared = exchange(1, totals, known_products, start_sum)
    values = weighted(1)
    for g in range(GROUPS):
        adjoint(g, values, g1)
        pack_edges(3, g, g1)
        send_edges(3, g)
        send_rows(3, g, g1)
    shared = share(1, collect(0, ar2, shared), ar1, 4 * mems, at_plane)
    for g in range(GROUPS):
        smooth(3, g, g1, v2)
    row = collect(1, ar1, shared)

    aa, ab, bb, ac, bc = (
        jnp.sum(jnp.where(lane1 == i, row, 0.0), axis=1, keepdims=True) for i in range(5)
    )
    first = aa / (aa + ab)
    rest = ab / (aa + ab)
    after = rest * rest * aa - 2.0 * rest * first * ab + first * first * bb
    along = rest + after / aa
    curved = along * along * (aa + ab) - along * first * (2.0 * ab + bb + ac) + first * first * (bb + bc)
    second = after / curved
    w0, w1 = first + second * along, -(second * first)
    q0, q1, q2 = rest - second * along, -first - second * (along - first), second * first
    for k in range(KL):
        a, b, c = v0[k], v1[k], v2[k]
        w_out[0, k] = w0 * a + w1 * b
        r_out[0, k] = q0 * a + q1 * b + q2 * c
    for kind, buffer in enumerate((rhalo, ehalo, rsbuf, rsbuf, dbuf, ar2, ar1)):
        wait_for(buffer, send_sem.at[kind])


def local(tiles, tcols, mems, right_side, perturbations, precision, covered):
    constants = [jnp.asarray(array) for array in filter_constants()]
    field = jax.ShapeDtypeStruct((1, KL, TY, TX), jnp.float32)
    f32 = jnp.float32
    pieces = TY // mems
    scratch = [
        pltpu.VMEM((KL, TY, TX), f32),
        pltpu.VMEM((KL, VL, TY, TX), BF16),
        pltpu.VMEM((VL, TY, TX), f32),
        pltpu.VMEM((2, 16), jnp.int32),
        *[pltpu.VMEM(array.shape, array.dtype) for array in constants],
        pltpu.VMEM((32, TX), f32),
        pltpu.VMEM((32, TX), f32),
        pltpu.VMEM((6, KL, TY, TX), f32),
        pltpu.VMEM((4, GROUPS, 2, KG, 8, TX), f32),
        pltpu.VMEM((4, GROUPS, 32, TX), f32),
        pltpu.VMEM((4, GROUPS, TY, TX), f32),
        pltpu.VMEM((2, 2, 128, HALF), f32),
        pltpu.VMEM((2, mems - 1, pieces, 2, 8, HALF), f32),
        pltpu.VMEM((2, 2, 128, HALF), f32),
        pltpu.VMEM((2, 128, HALF), f32),
        pltpu.VMEM((2, 128, HALF), f32),
        pltpu.VMEM((2, mems - 1, pieces, 8, HALF), f32),
        pltpu.VMEM((2, 1, HALF), f32),
        pltpu.VMEM((4 * mems - 1, 1, HALF), f32),
        pltpu.VMEM((tiles // 4 - 1, 1, HALF), f32),
        pltpu.SemaphoreType.DMA((9,)),
        pltpu.SemaphoreType.DMA((7,)),
        pltpu.SemaphoreType.DMA((4, GROUPS)),
        pltpu.SemaphoreType.DMA((4, GROUPS)),
        pltpu.SemaphoreType.DMA((2,)),
        pltpu.SemaphoreType.DMA((2,)),
        pltpu.SemaphoreType.DMA((2,)),
        pltpu.SemaphoreType.DMA((2,)),
    ]
    results = pl.pallas_call(
        functools.partial(kernel, tiles, tcols, mems),
        out_shape=(field, field),
        in_specs=[pl.BlockSpec(memory_space=pltpu.MemorySpace.HBM)] * 9,
        out_specs=(pl.BlockSpec(memory_space=pltpu.MemorySpace.VMEM),) * 2,
        scratch_shapes=scratch,
        compiler_params=pltpu.CompilerParams(
            collective_id=0, has_side_effects=True, vmem_limit_bytes=40 * 2**20
        ),
        name="conjugate_gradients",
    )(*[pltpu.with_memory_space_constraint(x, pltpu.MemorySpace.HBM) for x in (right_side, perturbations, precision, covered, *constants)])
    return pl.pallas_call(
        put_out,
        out_shape=(field, field),
        in_specs=[pl.BlockSpec(memory_space=pltpu.MemorySpace.VMEM)] * 2,
        out_specs=(pl.BlockSpec(memory_space=pltpu.MemorySpace.HBM),) * 2,
        scratch_shapes=[pltpu.SemaphoreType.DMA((2,))],
        compiler_params=pltpu.CompilerParams(vmem_limit_bytes=2**20),
        name="put_out",
    )(*results)


def put_out(w_in, r_in, w_out, r_out, sem):
    copies = [pltpu.make_async_copy(a, b, sem.at[i]) for i, (a, b) in enumerate(((w_in, w_out), (r_in, r_out)))]
    for copy in copies:
        copy.start()
    for copy in copies:
        copy.wait()


def solution(mesh, tcols=8):
    in_specs = (
        P("tile", "mem", None, None),
        P("tile", "mem", None, None, None),
        P("tile", None, None, None),
        P("tile", None, None),
    )
    out_specs = (P("tile", "mem", None, None),) * 2
    body = functools.partial(local, mesh.shape["tile"], tcols, mesh.shape["mem"])
    return jax.shard_map(body, mesh=mesh, in_specs=in_specs, out_specs=out_specs, check_vma=False)
```

```python
import functools

import jax
import jax.numpy as jnp
import numpy as np
from jax import lax
from jax.experimental import pallas as pl
from jax.experimental.pallas import tpu as pltpu
from jax.sharding import PartitionSpec as P

TY = 16
TX = 256
VL = 6
KL = 16
HALF = 128
GROUPS = 2
KG = KL // GROUPS
F32 = jnp.float32
BF16 = jnp.bfloat16


def three(matrix, dim):
    high = matrix.astype(BF16)
    low = (matrix - high.astype(np.float32)).astype(BF16)
    return np.concatenate([high, low, high] if dim else [high, high, low], axis=dim)


def filter_constants():
    j = np.arange(-8, 9).astype(np.float64)
    taps = (np.exp(-j * j / 32.0) / np.sqrt(np.sum(np.exp(-j * j / 16.0)))).astype(np.float32)

    def tap(offset):
        return np.where(np.abs(offset) <= 8, taps[np.clip(offset + 8, 0, 16)], np.float32(0))

    y = np.arange(TY)
    own = tap(y[None, :] - y[:, None])
    above = tap(np.arange(-8, 0)[None, :] - y[:, None])
    below = tap(np.arange(16, 24)[None, :] - y[:, None])
    eye = np.eye(KG, dtype=np.float32)
    rows = np.concatenate(
        [three(np.kron(eye, own), 1), three(np.concatenate([np.kron(eye, above), np.kron(eye, below)], axis=1), 1)], axis=1
    )
    strip = three(np.concatenate([above, own, below], axis=1), 1)
    x = np.arange(TX)
    columns = three(tap(x[:, None] - x[None, :]), 0)
    c = np.arange(8)
    eye16 = np.eye(16, dtype=np.float32)
    none = np.zeros((HALF, HALF), np.float32)
    left = np.kron(eye16, tap((c[:, None] - 8) - c[None, :]))
    right = np.kron(eye16, tap((c[:, None] + 8) - c[None, :]))
    edges = three(np.block([[left, none], [none, right]]), 0)
    spread = (np.arange(16)[:, None] == x[None, :] // 16).astype(np.float32)
    return rows, columns, edges, strip, spread


def split(value):
    high = value.astype(BF16)
    return high, (value - high.astype(F32)).astype(BF16)


def left_product(constant, value):
    high, low = split(value)
    return jnp.dot(constant, jnp.concatenate([high, high, low], axis=0), preferred_element_type=F32)


def right_product(value, constant):
    high, low = split(value)
    return jnp.dot(jnp.concatenate([high, low, high], axis=1), constant, preferred_element_type=F32)


def kernel(
    tiles, tcols, mems,
    src_hbm, pert_hbm, prec_hbm, cov_hbm, rows_hbm, columns_hbm, edges_hbm, strip_hbm, spread_hbm,
    w_out, r_out,
    v0, pert, obsw, cov, rows, columns, edges, strip, spread, fmask, tmask,
    fields, rhalo, ehalo, packs, inc, rsbuf, agbuf, wrows, dinc, dbuf, stat, ar1, ar2,
    load_sem, send_sem, rows_recv, edges_recv, rs_recv, ag_recv, d_recv, ar_recv,
):
    t = lax.axis_index("tile")
    m = lax.axis_index("mem")
    depth = tiles // 4

    def at_tile(offset):
        return {"tile": lax.rem(t + (offset + tiles), tiles), "mem": m}

    def at_mem(offset):
        return {"tile": t, "mem": lax.rem(m + offset, mems)}

    def at_plane(offset):
        q = lax.rem(t, 4)
        return {"tile": t - q + lax.rem(q + offset // mems, 4), "mem": lax.rem(m + offset % mems, mems)}

    def at_depth(offset):
        return {"tile": lax.rem(t + 4 * offset, tiles), "mem": m}

    neighbours = (tcols, -tcols, 1, -1, tcols + 1, -tcols - 1, tcols - 1, 1 - tcols)
    barrier = pltpu.get_barrier_semaphore()
    greeted = [at_tile(d) for d in neighbours] + [at_mem(d) for d in range(1, mems)]
    for device in greeted:
        pl.semaphore_signal(barrier, inc=1, device_id=device, device_id_type=pl.DeviceIdType.MESH)

    loads = []
    for i, (source, target) in enumerate(
        (
            (src_hbm.at[0], v0), (pert_hbm.at[0], pert), (prec_hbm.at[0], obsw), (cov_hbm.at[0], cov),
            (rows_hbm, rows), (columns_hbm, columns), (edges_hbm, edges), (strip_hbm, strip), (spread_hbm, spread),
        )
    ):
        copy = pltpu.make_async_copy(source, target, load_sem.at[i])
        copy.start()
        loads.append(copy)

    def remote(source, target, kind, recv, device):
        pltpu.make_async_remote_copy(
            src_ref=source, dst_ref=target, send_sem=send_sem.at[kind], recv_sem=recv,
            device_id=device, device_id_type=pl.DeviceIdType.MESH,
        ).start()

    def wait_for(buffer, semaphore):
        pltpu.make_async_copy(buffer, buffer, semaphore).wait()

    lane = lax.broadcasted_iota(jnp.int32, (TY, HALF), 1)

    def members(g):
        return pl.ds(KG * g, KG)

    def send_rows(n, g, source):
        remote(source.at[members(g), pl.ds(8, 8), :], rhalo.at[n, g, 0], 0, rows_recv.at[n, g], at_tile(tcols))
        remote(source.at[members(g), pl.ds(0, 8), :], rhalo.at[n, g, 1], 0, rows_recv.at[n, g], at_tile(-tcols))

    def pack_edges(n, g, field):
        packed_l = jnp.zeros((TY, HALF), F32)
        packed_r = jnp.zeros((TY, HALF), F32)
        for i in range(KG):
            here = lane // 8 == i
            value_l = field[KG * g + i, :, 0:HALF]
            value_l = pltpu.roll(value_l, 8 * i, 1) if i else value_l
            value_r = pltpu.roll(field[KG * g + i, :, HALF:TX], 8 * i + 8, 1)
            packed_l = jnp.where(here, value_l, packed_l)
            packed_r = jnp.where(here, value_r, packed_r)
        packs[n, g, :, 0:HALF] = packed_l
        packs[n, g, :, HALF:TX] = packed_r

    def send_edges(n, g):
        left, right = pl.ds(0, HALF), pl.ds(HALF, HALF)
        top, bottom, whole = pl.ds(0, 8), pl.ds(8, 8), pl.ds(0, TY)
        for rows_sent, side, place, half, offset in (
            (bottom, right, 0, left, tcols + 1), (top, left, 24, right, -tcols - 1),
            (bottom, left, 0, right, tcols - 1), (top, right, 24, left, 1 - tcols),
            (whole, right, 8, left, 1), (whole, left, 8, right, -1),
        ):
            height = TY if place == 8 else 8
            remote(
                packs.at[n, g, rows_sent, side], ehalo.at[n, g, pl.ds(place, height), half],
                1, edges_recv.at[n, g], at_tile(offset),
            )

    def flags(offset):
        s = lax.rem(t + (offset + tiles), tiles)
        return (s >= tcols).astype(F32), (s < tiles - tcols).astype(F32)

    here_top, here_bottom = flags(0)

    def smooth(n, g, field, target):
        partial = left_product(rows[:, : 3 * HALF], field[members(g)].reshape(KG * TY, TX))
        wait_for(ehalo.at[n, g], edges_recv.at[n, g])
        edge = right_product(left_product(strip[...], ehalo[n, g] * fmask[...]), edges[...])
        wait_for(rhalo.at[n, g], rows_recv.at[n, g])
        halo = jnp.concatenate(
            [rhalo[n, g, 0].reshape(KG * 8, TX) * here_top, rhalo[n, g, 1].reshape(KG * 8, TX) * here_bottom], axis=0
        )
        filtered = right_product(partial + left_product(rows[:, 3 * HALF :], halo), columns[...])
        edge_l, edge_r = edge[:, :HALF], edge[:, HALF:]
        for i in range(KG):
            k = KG * g + i
            part = filtered[TY * i : TY * i + TY]
            add_l = pltpu.roll(edge_l, HALF - 8 * i, 1) if i else edge_l
            add_r = pltpu.roll(edge_r, 120 - 8 * i, 1)
            target[k, :, 0:HALF] = part[:, :HALF] + jnp.where(lane < 8, add_l, 0.0)
            target[k, :, HALF:TX] = part[:, HALF:] + jnp.where(lane >= 120, add_r, 0.0)

    def corners(n, g):
        return right_product(left_product(strip[...], ehalo[n, g] * tmask[...]), edges[...])

    def gathered(field, g, totals):
        def body(k, totals):
            value = field[k]
            return tuple(totals[v] + pert[k, v].astype(F32) * value for v in range(VL))

        return lax.fori_loop(KG * g, KG * g + KG, body, totals)

    pieces = TY // mems

    def rows_of(y):
        return pl.ds(pl.multiple_of(8 * y, 8), VL)

    def send_corners(n, twist):
        def body(i, totals):
            for g in range(GROUPS):
                k = KG * g + i
                turn = lax.rem(HALF - 8 * i, HALF)
                add_l = jnp.where(lane < 8, pltpu.roll(twist[g][:, :HALF], turn, 1), 0.0)
                add_r = jnp.where(lane >= 120, pltpu.roll(twist[g][:, HALF:], 120 - 8 * i, 1), 0.0)
                totals = tuple(
                    totals[v]
                    + pert[k, v, :, 0:HALF].astype(F32) * add_l
                    + pert[k, v, :, HALF:TX].astype(F32) * add_r
                    for v in range(VL)
                )
            return totals

        totals = lax.fori_loop(0, KG, body, (jnp.zeros((TY, HALF), F32),) * VL)
        for v in range(VL):
            dinc[n, pl.ds(v, TY, stride=8), :] = totals[v]
        for d in range(1, mems):
            for piece in range(pieces):
                remote(
                    dinc.at[n, rows_of(lax.rem(m + d, mems) * pieces + piece), :], dbuf.at[n, d - 1, piece],
                    4, d_recv.at[n], at_mem(d),
                )

    def exchange(n, totals, meanwhile, ready):
        for v in range(VL):
            for h in range(2):
                inc[n, h, pl.ds(v, TY, stride=8), :] = totals[v][:, HALF * h : HALF * h + HALF]
        for d in range(1, mems):
            there = lax.rem(m + d, mems)
            for piece in range(pieces):
                remote(
                    inc.at[n, :, rows_of(there * pieces + piece), :], rsbuf.at[n, d - 1, piece],
                    2, rs_recv.at[n], at_mem(d),
                )
        result = meanwhile()
        wait_for(rsbuf.at[n], rs_recv.at[n])
        for piece in range(pieces):
            mine = rows_of(m * pieces + piece)
            total = inc[n, :, mine, :]
            for d in range(1, mems):
                total = total + rsbuf[n, d - 1, piece]
            agbuf[n, :, mine, :] = total
        for d in range(1, mems):
            for piece in range(pieces):
                mine = rows_of(m * pieces + piece)
                remote(agbuf.at[n, :, mine, :], agbuf.at[n, :, mine, :], 3, ag_recv.at[n], at_mem(d))
        result = ready(result)
        wait_for(rsbuf.at[n], ag_recv.at[n])
        return result

    def weighted(n):
        values = []
        for v in range(VL):
            halves = [agbuf[n, h, pl.ds(v, TY, stride=8), :] for h in range(2)]
            values.append(obsw[v] * jnp.concatenate(halves, axis=1))
        return values

    def adjoint(g, values, target):
        def body(k, carry):
            total = pert[k, 0].astype(F32) * values[0]
            for v in range(1, VL):
                total = total + pert[k, v].astype(F32) * values[v]
            target[k] = total
            return carry

        lax.fori_loop(KG * g, KG * g + KG, body, 0)

    g0, g1, u0, u1, v1, v2 = (fields.at[i] for i in range(6))
    zeros = (jnp.zeros((TY, TX), F32),) * VL

    loads[0].wait()
    for g in range(GROUPS):
        pack_edges(0, g, v0)
    for copy in loads[1:]:
        copy.wait()
    row8 = lax.broadcasted_iota(jnp.int32, (32, TX), 0)
    is_left = lax.broadcasted_iota(jnp.int32, (32, TX), 1) < HALF

    def masked(top, bottom):
        return jnp.where(row8 < 8, top, jnp.where(row8 >= 24, bottom, 1.0))

    mask = jnp.where(is_left, masked(*flags(-1)), masked(*flags(1)))
    fmask[...] = mask
    tmask[...] = masked(here_top, here_bottom) - mask
    for buffer in (inc, wrows, dinc):
        buffer[...] = jnp.zeros_like(buffer)
    mask = jnp.dot(cov[...].astype(F32), spread[...], preferred_element_type=F32)
    mask = jnp.concatenate([jnp.broadcast_to(mask[i : i + 1], (8, TX)) for i in range(2)], axis=0)
    for v in range(VL):
        obsw[v] = obsw[v] * mask
        for h in range(2):
            wrows[h, pl.ds(v, TY, stride=8), :] = obsw[v, :, HALF * h : HALF * h + HALF]

    pl.semaphore_wait(barrier, len(greeted))
    for g in range(GROUPS):
        send_edges(0, g)
    for g in range(GROUPS):
        send_rows(0, g, src_hbm.at[0])
    totals = zeros
    for g in range(GROUPS):
        smooth(0, g, v0, u0)
        totals = gathered(u0, g, totals)
    def corner_sums(n):
        send_corners(n, [corners(2 * n, g) for g in range(GROUPS)])

    exchange(0, totals, lambda: corner_sums(0), lambda result: None)
    values = weighted(0)
    for g in range(GROUPS):
        adjoint(g, values, g0)
        pack_edges(1, g, g0)
        send_edges(1, g)
        send_rows(1, g, g0)
    for g in range(GROUPS):
        smooth(1, g, g0, v1)
        pack_edges(2, g, v1)
        send_edges(2, g)
        send_rows(2, g, v1)
    totals = zeros
    for g in range(GROUPS):
        smooth(2, g, v1, u1)
        totals = gathered(u1, g, totals)

    def lines(totals):
        return [jnp.sum(total[:, :HALF] + total[:, HALF:], axis=0, keepdims=True) for total in totals]

    def known_products():
        def body(k, totals):
            a, b = v0[k], v1[k]
            return totals[0] + a * a, totals[1] + a * b, totals[2] + b * b

        corner_sums(1)
        return lines(lax.fori_loop(0, KL, body, zeros[:3]))

    lane1 = lax.broadcasted_iota(jnp.int32, (1, HALF), 1)

    def share(stage, row, buffer, count, place):
        stat[stage] = row
        for d in range(1, count):
            remote(stat.at[stage], buffer.at[d - 1], 5 + stage, ar_recv.at[stage], place(d))
        return row

    def collect(stage, buffer, row):
        wait_for(buffer, ar_recv.at[stage])
        return row + jnp.sum(buffer[...], axis=0)

    def start_sum(sums):
        for n in range(2):
            wait_for(dbuf.at[n], d_recv.at[n])
        crossed = [jnp.zeros((VL, HALF), F32)] * 2
        lane8 = lax.broadcasted_iota(jnp.int32, (VL, HALF), 1)
        for piece in range(pieces):
            mine = rows_of(m * pieces + piece)
            value = [wrows[h, mine, :] * agbuf[1, h, mine, :] for h in range(2)]
            outer = jnp.where(lane8 < 8, value[0], jnp.where(lane8 >= 120, value[1], 0.0))
            for n in range(2):
                corner = dinc[n, mine, :]
                for d in range(1, mems):
                    corner = corner + dbuf[n, d - 1, piece]
                crossed[n] = crossed[n] + (
                    agbuf[n, 0, mine, :] * value[0] + agbuf[n, 1, mine, :] * value[1] + corner * outer
                )
        row = jnp.zeros((1, HALF), F32)
        for i, line in enumerate(sums + [jnp.sum(total, axis=0, keepdims=True) for total in crossed]):
            row = jnp.where(lane1 == i, jnp.sum(line, axis=1, keepdims=True), row)
        return share(0, row, ar2, depth, at_depth)

    shared = exchange(1, totals, known_products, start_sum)
    values = weighted(1)
    for g in range(GROUPS):
        adjoint(g, values, g1)
        pack_edges(3, g, g1)
        send_edges(3, g)
        send_rows(3, g, g1)
    shared = share(1, collect(0, ar2, shared), ar1, 4 * mems, at_plane)
    for g in range(GROUPS):
        smooth(3, g, g1, v2)
    row = collect(1, ar1, shared)

    aa, ab, bb, ac, bc = (
        jnp.sum(jnp.where(lane1 == i, row, 0.0), axis=1, keepdims=True) for i in range(5)
    )
    first = aa / (aa + ab)
    rest = ab / (aa + ab)
    after = rest * rest * aa - 2.0 * rest * first * ab + first * first * bb
    along = rest + after / aa
    curved = along * along * (aa + ab) - along * first * (2.0 * ab + bb + ac) + first * first * (bb + bc)
    second = after / curved
    w0, w1 = first + second * along, -(second * first)
    q0, q1, q2 = rest - second * along, -first - second * (along - first), second * first
    for k in range(KL):
        a, b, c = v0[k], v1[k], v2[k]
        w_out[0, k] = w0 * a + w1 * b
        r_out[0, k] = q0 * a + q1 * b + q2 * c
    for kind, buffer in enumerate((rhalo, ehalo, rsbuf, rsbuf, dbuf, ar2, ar1)):
        wait_for(buffer, send_sem.at[kind])


def local(tiles, tcols, mems, right_side, perturbations, precision, covered):
    constants = [jnp.asarray(array) for array in filter_constants()]
    field = jax.ShapeDtypeStruct((1, KL, TY, TX), jnp.float32)
    f32 = jnp.float32
    pieces = TY // mems
    scratch = [
        pltpu.VMEM((KL, TY, TX), f32),
        pltpu.VMEM((KL, VL, TY, TX), BF16),
        pltpu.VMEM((VL, TY, TX), f32),
        pltpu.VMEM((2, 16), jnp.int32),
        *[pltpu.VMEM(array.shape, array.dtype) for array in constants],
        pltpu.VMEM((32, TX), f32),
        pltpu.VMEM((32, TX), f32),
        pltpu.VMEM((6, KL, TY, TX), f32),
        pltpu.VMEM((4, GROUPS, 2, KG, 8, TX), f32),
        pltpu.VMEM((4, GROUPS, 32, TX), f32),
        pltpu.VMEM((4, GROUPS, TY, TX), f32),
        pltpu.VMEM((2, 2, 128, HALF), f32),
        pltpu.VMEM((2, mems - 1, pieces, 2, VL, HALF), f32),
        pltpu.VMEM((2, 2, 128, HALF), f32),
        pltpu.VMEM((2, 128, HALF), f32),
        pltpu.VMEM((2, 128, HALF), f32),
        pltpu.VMEM((2, mems - 1, pieces, VL, HALF), f32),
        pltpu.VMEM((2, 1, HALF), f32),
        pltpu.VMEM((4 * mems - 1, 1, HALF), f32),
        pltpu.VMEM((tiles // 4 - 1, 1, HALF), f32),
        pltpu.SemaphoreType.DMA((9,)),
        pltpu.SemaphoreType.DMA((7,)),
        pltpu.SemaphoreType.DMA((4, GROUPS)),
        pltpu.SemaphoreType.DMA((4, GROUPS)),
        pltpu.SemaphoreType.DMA((2,)),
        pltpu.SemaphoreType.DMA((2,)),
        pltpu.SemaphoreType.DMA((2,)),
        pltpu.SemaphoreType.DMA((2,)),
    ]
    results = pl.pallas_call(
        functools.partial(kernel, tiles, tcols, mems),
        out_shape=(field, field),
        in_specs=[pl.BlockSpec(memory_space=pltpu.MemorySpace.HBM)] * 9,
        out_specs=(pl.BlockSpec(memory_space=pltpu.MemorySpace.VMEM),) * 2,
        scratch_shapes=scratch,
        compiler_params=pltpu.CompilerParams(
            collective_id=0, has_side_effects=True, vmem_limit_bytes=40 * 2**20
        ),
        name="conjugate_gradients",
    )(*[pltpu.with_memory_space_constraint(x, pltpu.MemorySpace.HBM) for x in (right_side, perturbations, precision, covered, *constants)])
    return pl.pallas_call(
        put_out,
        out_shape=(field, field),
        in_specs=[pl.BlockSpec(memory_space=pltpu.MemorySpace.VMEM)] * 2,
        out_specs=(pl.BlockSpec(memory_space=pltpu.MemorySpace.HBM),) * 2,
        scratch_shapes=[pltpu.SemaphoreType.DMA((2,))],
        compiler_params=pltpu.CompilerParams(vmem_limit_bytes=2**20),
        name="put_out",
    )(*results)


def put_out(w_in, r_in, w_out, r_out, sem):
    copies = [pltpu.make_async_copy(a, b, sem.at[i]) for i, (a, b) in enumerate(((w_in, w_out), (r_in, r_out)))]
    for copy in copies:
        copy.start()
    for copy in copies:
        copy.wait()


def solution(mesh, tcols=8):
    in_specs = (
        P("tile", "mem", None, None),
        P("tile", "mem", None, None, None),
        P("tile", None, None, None),
        P("tile", None, None),
    )
    out_specs = (P("tile", "mem", None, None),) * 2
    body = functools.partial(local, mesh.shape["tile"], tcols, mesh.shape["mem"])
    return jax.shard_map(body, mesh=mesh, in_specs=in_specs, out_specs=out_specs, check_vma=False)
```
